128 devices in a mesh: expert: 32 (over y, z, core), rep: 4 (over x).
Axes of the slice: x: 4, y: 4, z: 4, core: 2. Of those that a mesh axis runs over, the one named last changes fastest.
Arguments:
- tokens: bfloat16 [16384, 1664], P(('expert', 'rep')), may hold values from -50 to 50
- grad_grid: bfloat16 [256, 256, 1664], P(('expert', 'rep')), may hold values from -18 to 18
- keep_order: int32 [256, 256], P(('expert', 'rep')), may hold values from 0 to 255, each once within a row
- expert_ids: int32 [16384, 2], P(('expert', 'rep')), may hold values from 0 to 31, all different within a row; in each aligned block of 128 rows (0 to 127, 128 to 255, ...) at most 10 rows name the same one
- norm_gain: float32 [1664], replicated, may hold values from 0.25 to 1.75
- norm_bias: float32 [1664], replicated, may hold values from -3 to 3
- router_weight: float32 [1664, 32], replicated, may hold values from -0.15625 to 0.15625
- w_in: bfloat16 [32, 1664, 4096], P('expert', None, 'rep'), may hold values from -0.15625 to 0.15625
- w_out: bfloat16 [32, 4096, 1664], P('expert', 'rep'), may hold values from -0.09375 to 0.09375
Outputs:
- grad_tokens: bfloat16 [16384, 1664], P(('expert', 'rep'))
- grad_w_in: float32 [32, 1664, 4096], P('expert', None, 'rep')
- grad_w_out: float32 [32, 4096, 1664], P('expert', 'rep')
- grad_router: float32 [1664, 32], replicated
- grad_gain: float32 [1664], replicated
- grad_bias: float32 [1664], replicated
The draws below stay inside these ranges and needn't reach their ends.
Inputs may be any that keep to these rules, and one draw needn't show every extreme that they name: `expert_ids`: each row names two different experts. Within the 128 rows of one device (aligned blocks) no expert is named more than 10 times, a bound that some block reaches. `keep_order`: each row is an order of the 256 patches of its image; its first 64 entries are the kept patches, in the order of the image's kept tokens.
All inputs are finite; a program needn't handle non-finite values.
Results may differ from the reference program's by a relative error of at most 0.0062.
Values may be sent and summed in bfloat16 or wider, within the bound.
A program may use at most 128 MiB of HBM per device.

```python
import math
import jax
import jax.numpy as jnp
import numpy as np
from jax import lax

D = 1664
FF = 4096
EXPERTS = 32
PATCHES = 256
KEEP = 64
TOK_DEV = 128
IMAGES = 256
TOKENS = 16384
CAP = 10
N_EXPERT = 32
N_REP = 4


def draw_tokens(key, part):
    key_rows, key_shift, key_body = jax.random.split(key, 3)
    row_scale = jnp.exp(jax.random.uniform(key_rows, (TOKENS, 1), jnp.float32, 0.0, math.log(10.0)))
    row_shift = jax.random.uniform(key_shift, (TOKENS, 1), jnp.float32, -1.0, 1.0)
    entries = jnp.clip(jax.random.normal(key_body, (TOKENS, D), jnp.float32), -4.0, 4.0)
    return (row_scale * (entries + row_shift)).astype(jnp.bfloat16)


def draw_grad_grid(key, part):
    key_body = jax.random.fold_in(key, 0)
    ramp = 1.0 + 2.0 * jnp.arange(IMAGES, dtype=jnp.float32)[:, None, None] / max(IMAGES - 1, 1)
    entries = jnp.clip(jax.random.normal(key_body, (IMAGES, PATCHES, D), jnp.float32), -4.0, 4.0)
    return (ramp * entries).astype(jnp.bfloat16)


def shard_levels(key, dims, cuts, least, high):
    gain = 1.0
    for axis_at, parts in cuts:
        heights = jax.random.uniform(jax.random.fold_in(jax.random.fold_in(key, 6), axis_at), (parts,), jnp.float32, least / len(cuts), high / len(cuts))
        gain = gain * jnp.repeat(jnp.exp(heights), dims[axis_at] // parts).reshape((-1,) + (1,) * (len(dims) - 1 - axis_at))
    return gain


def assign_block(stream_key, own, number, rows, number_of, top, reach, skew):
    order = jax.random.permutation(stream_key, number_of)
    heavy_load, usual = load_shares(number_of, rows * top, reach, skew, True), load_shares(number_of, rows * top, reach, skew, False)
    places = jnp.arange(number_of)

    def named(lengths, turn):
        used = int((lengths > 0).sum())
        fixed = max(1, used // 4)
        passed = fixed + (places - fixed + turn * (used - fixed)) % max(1, number_of - fixed)
        return jnp.zeros((number_of,), jnp.int32).at[order[jnp.where(places < fixed, places, passed)]].set(jnp.asarray(lengths, jnp.int32))

    lengths = jnp.where(number % 4 == 0, named(heavy_load, number // 4), named(usual, number - number // 4 - 1))
    mixed = jax.random.permutation(jax.random.fold_in(own, 3), number_of)
    giver, receiver = mixed[0:number_of // 2 * 2:2], mixed[1:number_of // 2 * 2:2]
    margin = jnp.minimum(lengths[giver] - 1, reach - lengths[receiver]) // 2
    margin = jnp.where((giver == order[0]) | (receiver == order[0]) | (lengths[receiver] == 0), 0, jnp.maximum(margin, 0))
    passed = jax.random.randint(jax.random.fold_in(own, 4), (number_of // 2,), 0, 1 << 20) % (margin + 1)
    lengths = lengths.at[giver].add(-passed).at[receiver].add(passed)
    members = jnp.searchsorted(jnp.cumsum(lengths), jnp.arange(rows * top), side="right").astype(jnp.int32)
    grid = members.reshape(top, rows).T
    grid = grid[jax.random.permutation(jax.random.fold_in(own, 1), rows)]
    turn = jax.random.randint(jax.random.fold_in(own, 2), (rows, 1), 0, top)
    return jnp.take_along_axis(grid, (jnp.arange(top)[None, :] + turn) % top, axis=1)


def load_shares(amount, total, most, slope, full):
    weights = [(1 << 20) // math.isqrt(rank ** slope) + 1 for rank in range(1, amount + 1)]
    largest = most if full else min(most, max(-(-total // amount), total * weights[0] // sum(weights)))
    least = 1 if total - largest >= amount - 1 else 0
    counts, spare = [largest] + [least] * (amount - 1), total - largest - least * (amount - 1)
    while spare > 0:
        movable = [i for i in range(1, amount) if counts[i] < largest] or [i for i in range(1, amount) if counts[i] < most]
        whole, left = sum([weights[i] for i in movable]), spare
        for i in movable:
            addition = min(most - counts[i], max(1, left * weights[i] // whole), spare)
            counts[i] = counts[i] + addition
            spare = spare - addition
    return np.array(counts)


def gaussian(key, extent, width, bound, cuts=(), kind=jnp.bfloat16):
    drawn = width * jax.random.normal(key, extent, jnp.float32)
    if cuts:
        drawn = drawn * shard_levels(key, extent, cuts, -0.22, 0.18)
    return jnp.clip(drawn, -bound, bound).astype(kind)


def setup_inputs(seed: int = 0) -> dict:
    key_of = jax.random.split(jax.random.key(seed), 10)
    tokens = draw_tokens(jax.random.fold_in(key_of[9], 71), 0)
    grad_grid = draw_grad_grid(jax.random.fold_in(key_of[9], 71), 0)
    keep_order = jax.vmap(lambda own: jax.random.permutation(own, PATCHES))(jax.random.split(key_of[2], IMAGES)).reshape((IMAGES, PATCHES)).astype(jnp.int32)
    expert_ids_keys = jax.random.split(jax.random.fold_in(key_of[3], 1), TOKENS // TOK_DEV)
    expert_ids_turns = jax.random.permutation(jax.random.fold_in(key_of[3], 3), TOKENS // TOK_DEV)
    expert_ids = jax.vmap(lambda own, number: assign_block(jax.random.fold_in(key_of[3], 2), own, number, TOK_DEV, EXPERTS, 2, CAP, 2))(expert_ids_keys, expert_ids_turns).reshape((TOKENS, 2))
    norm_gain = jnp.clip(1.0 + 0.15 * jax.random.normal(key_of[4], (D,), jnp.float32), 0.25, 1.75)
    norm_bias = gaussian(key_of[5], (D,), 0.5, 3.0, (), jnp.float32)
    router_weight = gaussian(key_of[6], (D, EXPERTS), D ** -0.5, 0.15625, (), jnp.float32)
    w_in = gaussian(key_of[7], (EXPERTS, D, FF), D ** -0.5, 0.15625, ((0, 32), (2, 4)))
    w_out = gaussian(key_of[8], (EXPERTS, FF, D), FF ** -0.5, 0.09375, ((0, 32), (1, 4)))
    return dict(tokens=tokens, grad_grid=grad_grid, keep_order=keep_order, expert_ids=expert_ids, norm_gain=norm_gain, norm_bias=norm_bias, router_weight=router_weight, w_in=w_in, w_out=w_out)


NORM_EPS = 1e-06
PRECISE = lax.Precision.HIGHEST

def gelu_parts(preact):
    normal_cdf = 0.5 * (1.0 + lax.erf(preact * 0.7071067811865476))
    density = jnp.exp(-0.5 * preact * preact) * 0.3989422804014327
    return (preact * normal_cdf, normal_cdf + preact * density)

def layer_norm(tokens, norm_gain, norm_bias):
    values = tokens.astype(jnp.float32)
    center = values - lax.optimization_barrier(jnp.mean(values, axis=1, keepdims=True))
    inverse = 1.0 / jnp.sqrt(lax.optimization_barrier(jnp.mean(center * center, axis=1, keepdims=True)) + NORM_EPS)
    normed = center * inverse
    return (normed, inverse, (normed * norm_gain + norm_bias).astype(jnp.bfloat16))

def gate_values(normed_in, router_weight, expert_ids):
    experts = router_weight.shape[1]
    logits = jnp.dot(normed_in.astype(jnp.float32), router_weight, precision=PRECISE)
    chosen = (expert_ids[:, :, None] == jnp.arange(experts, dtype=jnp.int32)[None, None, :]).astype(jnp.float32)
    picked = lax.optimization_barrier(jnp.sum(logits[:, None, :] * chosen, axis=2))
    first_gate = jax.nn.sigmoid(picked[:, 0] - picked[:, 1])
    second_gate = jax.nn.sigmoid(picked[:, 1] - picked[:, 0])
    return (chosen, first_gate, second_gate)

def expert_rows(normed_rows, grad_rows, gate_rows, weight_in, weight_out):
    preact = jnp.dot(normed_rows, weight_in, preferred_element_type=jnp.float32)
    hidden, hidden_slope = gelu_parts(preact)
    gate_col = gate_rows.astype(jnp.float32)[:, None]
    weighted = (gate_col * hidden).astype(jnp.bfloat16)
    back_hidden = jnp.dot(grad_rows, weight_out.T, preferred_element_type=jnp.float32)
    gate_grad = lax.optimization_barrier(jnp.sum(back_hidden * hidden, axis=1))
    pre_grad = (gate_col * back_hidden * hidden_slope).astype(jnp.bfloat16)
    grad_out = jnp.dot(weighted.T, grad_rows, preferred_element_type=jnp.float32)
    grad_in = jnp.dot(normed_rows.T, pre_grad, preferred_element_type=jnp.float32)
    input_grad = jnp.dot(pre_grad, weight_in.T, preferred_element_type=jnp.float32)
    return (input_grad, gate_grad, grad_in, grad_out)

def reference(tokens, grad_grid, keep_order, expert_ids, norm_gain, norm_bias, router_weight, w_in, w_out):
    devices = N_EXPERT * N_REP
    grad_kept = jnp.take_along_axis(grad_grid, keep_order[:, :KEEP, None].astype(jnp.int32), axis=1).reshape(TOKENS, D)
    normed, inverse, normed_in = layer_norm(tokens, norm_gain, norm_bias)
    chosen, first_gate, second_gate = gate_values(normed_in, router_weight, expert_ids)
    gate_half = jnp.stack([first_gate, second_gate], axis=1).astype(jnp.bfloat16)
    expert_hits = lax.optimization_barrier(jnp.sum(chosen, axis=1)).reshape(devices, TOK_DEV, EXPERTS)
    before = (jnp.cumsum(expert_hits, axis=1) - expert_hits).reshape(TOKENS, EXPERTS)
    slot_place = lax.optimization_barrier(jnp.sum(before[:, None, :] * chosen, axis=2)).astype(jnp.int32)
    slot_index = expert_ids.astype(jnp.int32) * CAP + slot_place
    owner = jnp.arange(TOKENS, dtype=jnp.int32) // TOK_DEV
    store_normed = jnp.zeros((devices, EXPERTS * CAP, D), jnp.bfloat16)
    store_grad = jnp.zeros((devices, EXPERTS * CAP, D), jnp.bfloat16)
    store_gate = jnp.zeros((devices, EXPERTS * CAP), jnp.bfloat16)
    for column in range(2):
        store_normed = store_normed.at[owner, slot_index[:, column]].set(normed_in)
        store_grad = store_grad.at[owner, slot_index[:, column]].set(grad_kept)
        store_gate = store_gate.at[owner, slot_index[:, column]].set(gate_half[:, column])

    def by_expert(store):
        tail = store.shape[2:]
        return jnp.swapaxes(store.reshape((devices, EXPERTS, CAP) + tail), 0, 1).reshape((EXPERTS, devices * CAP) + tail)

    def by_device(store):
        tail = store.shape[2:]
        return jnp.swapaxes(store.reshape((EXPERTS, devices, CAP) + tail), 0, 1).reshape((devices, EXPERTS * CAP) + tail)

    def one_expert(inputs):
        rows_normed, rows_grad, rows_gate, weight_in, weight_out = inputs
        return expert_rows(rows_normed, rows_grad, rows_gate, weight_in, weight_out)
    input_grad, gate_grad, grad_w_in, grad_w_out = lax.map(one_expert, (by_expert(store_normed), by_expert(store_grad), by_expert(store_gate), w_in, w_out))
    back_rows = by_device(input_grad)
    back_gate = by_device(gate_grad)
    mixed_grad = back_rows[owner, slot_index[:, 0]] + back_rows[owner, slot_index[:, 1]]
    gate_grads = jnp.stack([back_gate[owner, slot_index[:, 0]], back_gate[owner, slot_index[:, 1]]], axis=1)
    logit_grad = first_gate * second_gate * (gate_grads[:, 0] - gate_grads[:, 1])
    logits_grad = logit_grad[:, None] * (chosen[:, 0] - chosen[:, 1])
    normed_grad = mixed_grad + jnp.dot(logits_grad, router_weight.T, precision=PRECISE)
    grad_router = jnp.dot(normed_in.astype(jnp.float32).T, logits_grad, precision=PRECISE)
    grad_gain = lax.optimization_barrier(jnp.sum(normed_grad * normed, axis=0))
    grad_bias = lax.optimization_barrier(jnp.sum(normed_grad, axis=0))
    scaled = normed_grad * norm_gain
    branch = inverse * (scaled - lax.optimization_barrier(jnp.mean(scaled, axis=1, keepdims=True)) - normed * lax.optimization_barrier(jnp.mean(scaled * normed, axis=1, keepdims=True)))
    grad_tokens = (grad_kept.astype(jnp.float32) + branch).astype(jnp.bfloat16)
    return (grad_tokens, grad_w_in, grad_w_out, grad_router, grad_gain, grad_bias)
```

```python
import jax
import jax.numpy as jnp
from jax import lax
from jax.sharding import PartitionSpec as P

NORM_EPS = 1e-06
PRECISE = lax.Precision.HIGHEST


def gelu_parts(preact):
    normal_cdf = 0.5 * (1.0 + lax.erf(preact * 0.7071067811865476))
    density = jnp.exp(-0.5 * preact * preact) * 0.3989422804014327
    return (preact * normal_cdf, normal_cdf + preact * density)


def contract(left, right, left_axis, right_axis):
    return lax.dot_general(
        left, right, (((left_axis,), (right_axis,)), ((), ())), preferred_element_type=jnp.float32
    )


def layer_norm(tokens, norm_gain, norm_bias):
    values = tokens.astype(jnp.float32)
    center = values - jnp.mean(values, axis=1, keepdims=True)
    inverse = 1.0 / jnp.sqrt(jnp.mean(center * center, axis=1, keepdims=True) + NORM_EPS)
    normed = center * inverse
    return (normed, inverse, (normed * norm_gain + norm_bias).astype(jnp.bfloat16))


def gate_values(normed_in, router_weight, expert_ids):
    experts = router_weight.shape[1]
    logits = jnp.dot(normed_in.astype(jnp.float32), router_weight, precision=PRECISE)
    chosen = (expert_ids[:, :, None] == jnp.arange(experts, dtype=jnp.int32)[None, None, :]).astype(
        jnp.float32
    )
    picked = jnp.sum(logits[:, None, :] * chosen, axis=2)
    first_gate = jax.nn.sigmoid(picked[:, 0] - picked[:, 1])
    second_gate = jax.nn.sigmoid(picked[:, 1] - picked[:, 0])
    return (chosen, first_gate, second_gate)


def expert_rows(normed_rows, grad_rows, gate_rows, weight_in, weight_out):
    preact = contract(normed_rows, weight_in, 1, 0)
    hidden, hidden_slope = gelu_parts(preact)
    gate_col = gate_rows.astype(jnp.float32)[:, None]
    weighted = (gate_col * hidden).astype(jnp.bfloat16)
    back_hidden = contract(grad_rows, weight_out, 1, 1)
    gate_grad = jnp.sum(back_hidden * hidden, axis=1)
    pre_grad = (gate_col * back_hidden * hidden_slope).astype(jnp.bfloat16)
    grad_out = contract(weighted, grad_rows, 0, 0)
    grad_in = contract(normed_rows, pre_grad, 0, 0)
    input_grad = contract(pre_grad, weight_in, 1, 1)
    return (input_grad, gate_grad, grad_in, grad_out)


def on_device(
    tokens, grad_grid, keep_order, expert_ids, norm_gain, norm_bias, router_weight, w_in, w_out
):
    experts = router_weight.shape[1]
    tok_count = tokens.shape[0]
    model_width = tokens.shape[1]
    capacity = 5 * tok_count // (2 * experts)
    kept_count = tok_count // grad_grid.shape[0]
    lane = 128
    grad_kept = jnp.take_along_axis(grad_grid, keep_order[:, :kept_count, None], axis=1).reshape(
        tok_count, model_width
    )
    normed, inverse, normed_in = layer_norm(tokens, norm_gain, norm_bias)
    chosen, first_gate, second_gate = gate_values(normed_in, router_weight, expert_ids)
    gate_half = jnp.stack([first_gate, second_gate], axis=1).astype(jnp.bfloat16)
    expert_hits = jnp.sum(chosen, axis=1)
    before = jnp.cumsum(expert_hits, axis=0) - expert_hits
    slot_place = jnp.sum(before[:, None, :] * chosen, axis=2).astype(jnp.int32)
    slot_index = expert_ids * capacity + slot_place
    slot_ids = jnp.arange(experts * capacity, dtype=jnp.int32)
    spread = (slot_index[:, :, None] == slot_ids[None, None, :]).astype(jnp.float32)
    assign = jnp.sum(spread, axis=1)
    assign_half = assign.astype(jnp.bfloat16)
    both = jnp.concatenate([normed_in, grad_kept], axis=1)
    send_rows = contract(assign_half, both, 0, 0).astype(jnp.bfloat16)
    send_gate = jnp.einsum(
        "tks,tk->s", spread, gate_half.astype(jnp.float32), precision=PRECISE
    ).astype(jnp.bfloat16)
    gate_block = jnp.concatenate(
        [send_gate[:, None], jnp.zeros((experts * capacity, lane - 1), jnp.bfloat16)], axis=1
    )
    send = jnp.concatenate([send_rows, gate_block], axis=1).reshape(experts, capacity, -1)
    got = lax.all_to_all(send, "expert", split_axis=0, concat_axis=0, tiled=True)
    got = lax.all_gather(got, "rep", axis=0, tiled=True)
    got = got.reshape(-1, got.shape[-1])
    input_grad, gate_grad, grad_in, grad_out = expert_rows(
        got[:, :model_width],
        got[:, model_width : 2 * model_width],
        got[:, 2 * model_width],
        w_in[0],
        w_out[0],
    )
    slots_all = input_grad.shape[0]
    packed = jnp.concatenate(
        [input_grad, gate_grad[:, None], jnp.zeros((slots_all, lane - 1), jnp.float32)], axis=1
    )
    copies = lax.axis_size("rep")
    packed = packed.reshape(copies, slots_all // copies, -1)
    back = lax.psum_scatter(packed, "rep", scatter_dimension=0, tiled=True)
    back = back.reshape(experts, capacity, -1)
    ret = lax.all_to_all(back, "expert", split_axis=0, concat_axis=0, tiled=True)
    ret = ret.reshape(experts * capacity, -1)
    ret_rows = ret[:, :model_width]
    ret_gate = ret[:, model_width]
    grad_w_in = grad_in[None]
    grad_w_out = grad_out[None]
    mixed_grad = jnp.dot(assign, ret_rows, precision=PRECISE)
    gate_grads = jnp.einsum("tks,s->tk", spread, ret_gate, precision=PRECISE)
    logit_grad = first_gate * second_gate * (gate_grads[:, 0] - gate_grads[:, 1])
    logits_grad = logit_grad[:, None] * (chosen[:, 0] - chosen[:, 1])
    normed_grad = mixed_grad + lax.dot_general(
        logits_grad, router_weight, (((1,), (1,)), ((), ())), precision=PRECISE
    )
    local_router = lax.dot_general(
        normed_in.astype(jnp.float32), logits_grad, (((0,), (0,)), ((), ())), precision=PRECISE
    )
    local_gain = jnp.sum(normed_grad * normed, axis=0)
    local_bias = jnp.sum(normed_grad, axis=0)
    summed = lax.psum(
        jnp.concatenate([local_router, local_gain[:, None], local_bias[:, None]], axis=1),
        ("expert", "rep"),
    )
    grad_router = summed[:, :experts]
    grad_gain = summed[:, experts]
    grad_bias = summed[:, experts + 1]
    scaled = normed_grad * norm_gain
    branch = inverse * (
        scaled
        - jnp.mean(scaled, axis=1, keepdims=True)
        - normed * jnp.mean(scaled * normed, axis=1, keepdims=True)
    )
    grad_tokens = (grad_kept.astype(jnp.float32) + branch).astype(jnp.bfloat16)
    return (grad_tokens, grad_w_in, grad_w_out, grad_router, grad_gain, grad_bias)


def solution(mesh):
    placed = (
        P(("expert", "rep"), None),
        P(("expert", "rep"), None, None),
        P(("expert", "rep"), None),
        P(("expert", "rep"), None),
        P(),
        P(),
        P(),
        P("expert", None, "rep"),
        P("expert", "rep", None),
    )
    return jax.shard_map(
        on_device,
        mesh=mesh,
        in_specs=placed,
        out_specs=(
            P(("expert", "rep"), None),
            P("expert", None, "rep"),
            P("expert", "rep", None),
            P(),
            P(),
            P(),
        ),
        check_vma=False,
    )
```

```python
import jax
import jax.numpy as jnp
from jax import lax
from jax.sharding import PartitionSpec as P

NORM_EPS = 1e-06
PRECISE = lax.Precision.HIGHEST


def gelu_parts(preact):
    normal_cdf = 0.5 * (1.0 + lax.erf(preact * 0.7071067811865476))
    density = jnp.exp(-0.5 * preact * preact) * 0.3989422804014327
    return (preact * normal_cdf, normal_cdf + preact * density)


def contract(left, right, left_axis, right_axis):
    return lax.dot_general(
        left, right, (((left_axis,), (right_axis,)), ((), ())), preferred_element_type=jnp.float32
    )


def layer_norm(tokens, norm_gain, norm_bias):
    values = tokens.astype(jnp.float32)
    center = values - jnp.mean(values, axis=1, keepdims=True)
    inverse = 1.0 / jnp.sqrt(jnp.mean(center * center, axis=1, keepdims=True) + NORM_EPS)
    normed = center * inverse
    return (normed, inverse, (normed * norm_gain + norm_bias).astype(jnp.bfloat16))


def gate_values(normed_in, router_weight, expert_ids):
    experts = router_weight.shape[1]
    logits = jnp.dot(normed_in.astype(jnp.float32), router_weight, precision=PRECISE)
    chosen = (expert_ids[:, :, None] == jnp.arange(experts, dtype=jnp.int32)[None, None, :]).astype(
        jnp.float32
    )
    picked = jnp.sum(logits[:, None, :] * chosen, axis=2)
    first_gate = jax.nn.sigmoid(picked[:, 0] - picked[:, 1])
    second_gate = jax.nn.sigmoid(picked[:, 1] - picked[:, 0])
    return (chosen, first_gate, second_gate)


def expert_rows(normed_rows, grad_rows, gate_rows, weight_in, weight_out):
    preact = contract(normed_rows, weight_in, 1, 0)
    hidden, hidden_slope = gelu_parts(preact)
    gate_col = gate_rows.astype(jnp.float32)[:, None]
    weighted = (gate_col * hidden).astype(jnp.bfloat16)
    back_hidden = contract(grad_rows, weight_out, 1, 1)
    gate_grad = jnp.sum(back_hidden * hidden, axis=1)
    pre_grad = (gate_col * back_hidden * hidden_slope).astype(jnp.bfloat16)
    grad_out = contract(weighted, grad_rows, 0, 0)
    grad_in = contract(normed_rows, pre_grad, 0, 0)
    input_grad = contract(pre_grad, weight_in, 1, 1)
    return (input_grad, gate_grad, grad_in, grad_out)


def all_sum(part):
    devices = lax.axis_size("expert") * lax.axis_size("rep")
    flat = part.reshape(-1)
    width = -(-flat.shape[0] // (devices * 128)) * 128
    flat = jnp.pad(flat, (0, devices * width - flat.shape[0]))
    pieces = lax.all_to_all(
        flat.reshape(devices, width), ("expert", "rep"), split_axis=0, concat_axis=0, tiled=True
    )
    mine = jnp.sum(pieces, axis=0)
    spread_out = jnp.broadcast_to(mine[None], (devices, width))
    whole = lax.all_to_all(spread_out, ("expert", "rep"), split_axis=0, concat_axis=0, tiled=True)
    return whole.reshape(-1)[: part.size].reshape(part.shape)


def on_device(
    tokens, grad_grid, keep_order, expert_ids, norm_gain, norm_bias, router_weight, w_in, w_out
):
    experts = router_weight.shape[1]
    tok_count = tokens.shape[0]
    model_width = tokens.shape[1]
    capacity = 5 * tok_count // (2 * experts)
    kept_count = tok_count // grad_grid.shape[0]
    lane = 128
    grad_kept = jnp.take_along_axis(grad_grid, keep_order[:, :kept_count, None], axis=1).reshape(
        tok_count, model_width
    )
    normed, inverse, normed_in = layer_norm(tokens, norm_gain, norm_bias)
    chosen, first_gate, second_gate = gate_values(normed_in, router_weight, expert_ids)
    gate_half = jnp.stack([first_gate, second_gate], axis=1).astype(jnp.bfloat16)
    expert_hits = jnp.sum(chosen, axis=1)
    before = jnp.cumsum(expert_hits, axis=0) - expert_hits
    slot_place = jnp.sum(before[:, None, :] * chosen, axis=2).astype(jnp.int32)
    slot_index = slot_place * experts + expert_ids
    slot_ids = jnp.arange(experts * capacity, dtype=jnp.int32)
    spread = (slot_index[:, :, None] == slot_ids[None, None, :]).astype(jnp.float32)
    assign = jnp.sum(spread, axis=1)
    assign_half = assign.astype(jnp.bfloat16)
    both = jnp.concatenate([normed_in, grad_kept], axis=1)
    send_rows = contract(assign_half, both, 0, 0).astype(jnp.bfloat16)
    send_gate = jnp.einsum(
        "tks,tk->s", spread, gate_half.astype(jnp.float32), precision=PRECISE
    ).astype(jnp.bfloat16)
    gate_block = jnp.concatenate(
        [send_gate[:, None], jnp.zeros((experts * capacity, lane - 1), jnp.bfloat16)], axis=1
    )
    send = jnp.concatenate([send_rows, gate_block], axis=1).reshape(capacity, experts, -1)
    got = lax.all_to_all(send, "expert", split_axis=1, concat_axis=1, tiled=True)
    got = lax.all_gather(got, "rep", axis=0, tiled=False)
    got = got.reshape(-1, got.shape[-1])
    input_grad, gate_grad, grad_in, grad_out = expert_rows(
        got[:, :model_width],
        got[:, model_width : 2 * model_width],
        got[:, 2 * model_width],
        w_in[0],
        w_out[0],
    )
    slots_all = input_grad.shape[0]
    packed = jnp.concatenate(
        [input_grad, gate_grad[:, None], jnp.zeros((slots_all, lane - 1), jnp.float32)], axis=1
    )
    copies = lax.axis_size("rep")
    packed = packed.reshape(copies, slots_all // copies, -1)
    back = lax.psum_scatter(packed, "rep", scatter_dimension=0, tiled=True)
    back = back.reshape(capacity, experts, -1)
    ret = lax.all_to_all(back, "expert", split_axis=1, concat_axis=1, tiled=True)
    ret = ret.reshape(experts * capacity, -1)
    ret_rows = ret[:, :model_width]
    ret_gate = ret[:, model_width]
    grad_w_in = grad_in[None]
    grad_w_out = grad_out[None]
    mixed_grad = jnp.dot(assign, ret_rows, precision=PRECISE)
    gate_grads = jnp.einsum("tks,s->tk", spread, ret_gate, precision=PRECISE)
    logit_grad = first_gate * second_gate * (gate_grads[:, 0] - gate_grads[:, 1])
    logits_grad = logit_grad[:, None] * (chosen[:, 0] - chosen[:, 1])
    normed_grad = mixed_grad + lax.dot_general(
        logits_grad, router_weight, (((1,), (1,)), ((), ())), precision=PRECISE
    )
    local_router = lax.dot_general(
        normed_in.astype(jnp.float32), logits_grad, (((0,), (0,)), ((), ())), precision=PRECISE
    )
    local_gain = jnp.sum(normed_grad * normed, axis=0)
    local_bias = jnp.sum(normed_grad, axis=0)
    summed = all_sum(
        jnp.concatenate([local_router, local_gain[:, None], local_bias[:, None]], axis=1)
    )
    grad_router = summed[:, :experts]
    grad_gain = summed[:, experts]
    grad_bias = summed[:, experts + 1]
    scaled = normed_grad * norm_gain
    branch = inverse * (
        scaled
        - jnp.mean(scaled, axis=1, keepdims=True)
        - normed * jnp.mean(scaled * normed, axis=1, keepdims=True)
    )
    grad_tokens = (grad_kept.astype(jnp.float32) + branch).astype(jnp.bfloat16)
    return (grad_tokens, grad_w_in, grad_w_out, grad_router, grad_gain, grad_bias)


def solution(mesh):
    placed = (
        P(("expert", "rep"), None),
        P(("expert", "rep"), None, None),
        P(("expert", "rep"), None),
        P(("expert", "rep"), None),
        P(),
        P(),
        P(),
        P("expert", None, "rep"),
        P("expert", "rep", None),
    )
    return jax.shard_map(
        on_device,
        mesh=mesh,
        in_specs=placed,
        out_specs=(
            P(("expert", "rep"), None),
            P("expert", None, "rep"),
            P("expert", "rep", None),
            P(),
            P(),
            P(),
        ),
        check_vma=False,
    )
```

```python
import jax
import jax.numpy as jnp
from jax import lax
from jax.sharding import PartitionSpec as P

NORM_EPS = 1e-06
PRECISE = lax.Precision.HIGHEST


def gelu_parts(preact):
    normal_cdf = 0.5 * (1.0 + lax.erf(preact * 0.7071067811865476))
    density = jnp.exp(-0.5 * preact * preact) * 0.3989422804014327
    return (preact * normal_cdf, normal_cdf + preact * density)


def contract(left, right, left_axis, right_axis):
    return lax.dot_general(
        left, right, (((left_axis,), (right_axis,)), ((), ())), preferred_element_type=jnp.float32
    )


def layer_norm(tokens, norm_gain, norm_bias):
    values = tokens.astype(jnp.float32)
    center = values - jnp.mean(values, axis=1, keepdims=True)
    inverse = 1.0 / jnp.sqrt(jnp.mean(center * center, axis=1, keepdims=True) + NORM_EPS)
    normed = center * inverse
    return (normed, inverse, (normed * norm_gain + norm_bias).astype(jnp.bfloat16))


def gate_values(normed_in, router_weight, expert_ids):
    experts = router_weight.shape[1]
    logits = jnp.dot(normed_in.astype(jnp.float32), router_weight, precision=PRECISE)
    chosen = (expert_ids[:, :, None] == jnp.arange(experts, dtype=jnp.int32)[None, None, :]).astype(
        jnp.float32
    )
    picked = jnp.sum(logits[:, None, :] * chosen, axis=2)
    first_gate = jax.nn.sigmoid(picked[:, 0] - picked[:, 1])
    second_gate = jax.nn.sigmoid(picked[:, 1] - picked[:, 0])
    return (chosen, first_gate, second_gate)


def expert_rows(normed_rows, grad_rows, gate_rows, weight_in, weight_out):
    preact = contract(normed_rows, weight_in, 1, 0)
    hidden, hidden_slope = gelu_parts(preact)
    gate_col = gate_rows.astype(jnp.float32)[:, None]
    weighted = (gate_col * hidden).astype(jnp.bfloat16)
    back_hidden = contract(grad_rows, weight_out, 1, 1)
    gate_grad = jnp.sum(back_hidden * hidden, axis=1)
    pre_grad = (gate_col * back_hidden * hidden_slope).astype(jnp.bfloat16)
    grad_out = contract(weighted, grad_rows, 0, 0)
    grad_in = contract(normed_rows, pre_grad, 0, 0)
    input_grad = contract(pre_grad, weight_in, 1, 1)
    return (input_grad, gate_grad, grad_in, grad_out)


def all_sum(part):
    devices = lax.axis_size("expert") * lax.axis_size("rep")
    flat = part.reshape(-1)
    width = -(-flat.shape[0] // (devices * 128)) * 128
    flat = jnp.pad(flat, (0, devices * width - flat.shape[0]))
    pieces = lax.all_to_all(
        flat.reshape(devices, width), ("expert", "rep"), split_axis=0, concat_axis=0, tiled=True
    )
    mine = jnp.sum(pieces, axis=0)
    spread_out = jnp.broadcast_to(mine[None], (devices, width))
    whole = lax.all_to_all(spread_out, ("expert", "rep"), split_axis=0, concat_axis=0, tiled=True)
    return whole.reshape(-1)[: part.size].reshape(part.shape)


def on_device(
    tokens, grad_grid, keep_order, expert_ids, norm_gain, norm_bias, router_weight, w_in, w_out
):
    experts = router_weight.shape[1]
    tok_count = tokens.shape[0]
    model_width = tokens.shape[1]
    capacity = 5 * tok_count // (2 * experts)
    kept_count = tok_count // grad_grid.shape[0]
    lane = 128
    grad_kept = jnp.take_along_axis(grad_grid, keep_order[:, :kept_count, None], axis=1).reshape(
        tok_count, model_width
    )
    normed, inverse, normed_in = layer_norm(tokens, norm_gain, norm_bias)
    chosen, first_gate, second_gate = gate_values(normed_in, router_weight, expert_ids)
    gate_half = jnp.stack([first_gate, second_gate], axis=1).astype(jnp.bfloat16)
    expert_hits = jnp.sum(chosen, axis=1)
    before = jnp.cumsum(expert_hits, axis=0) - expert_hits
    slot_place = jnp.sum(before[:, None, :] * chosen, axis=2).astype(jnp.int32)
    slot_index = slot_place * experts + expert_ids
    slot_ids = jnp.arange(experts * capacity, dtype=jnp.int32)
    spread = (slot_index[:, :, None] == slot_ids[None, None, :]).astype(jnp.float32)
    assign = jnp.sum(spread, axis=1)
    assign_half = assign.astype(jnp.bfloat16)
    both = jnp.concatenate([normed_in, grad_kept], axis=1)
    send_rows = contract(assign_half, both, 0, 0).astype(jnp.bfloat16)
    send_gate = jnp.einsum(
        "tks,tk->s", spread, gate_half.astype(jnp.float32), precision=PRECISE
    ).astype(jnp.bfloat16)
    gate_block = jnp.concatenate(
        [send_gate[:, None], jnp.zeros((experts * capacity, lane - 1), jnp.bfloat16)], axis=1
    )
    send = jnp.concatenate([send_rows, gate_block], axis=1).reshape(capacity, experts, -1)
    got = lax.all_to_all(send, "expert", split_axis=1, concat_axis=1, tiled=True)
    got = lax.all_gather(got, "rep", axis=0, tiled=False)
    got = got.reshape(-1, got.shape[-1])
    input_grad, gate_grad, grad_in, grad_out = expert_rows(
        got[:, :model_width],
        got[:, model_width : 2 * model_width],
        got[:, 2 * model_width],
        w_in[0],
        w_out[0],
    )
    slots_all = input_grad.shape[0]
    rep_at = lax.axis_index("rep")
    gate_hi = gate_grad.astype(jnp.bfloat16)
    gate_lo = (gate_grad - gate_hi.astype(jnp.float32)).astype(jnp.bfloat16)
    cols = jnp.arange(lane, dtype=jnp.int32)[None, :]
    zero = jnp.zeros((), jnp.bfloat16)
    gate_cols = jnp.where(
        cols == 2 * rep_at,
        gate_hi[:, None],
        jnp.where(cols == 2 * rep_at + 1, gate_lo[:, None], zero),
    )
    packed = jnp.concatenate([input_grad.astype(jnp.bfloat16), gate_cols], axis=1)
    copies = lax.axis_size("rep")
    packed = packed.reshape(copies, slots_all // copies, -1)
    back = lax.psum_scatter(packed, "rep", scatter_dimension=0, tiled=True)
    back = back.reshape(capacity, experts, -1)
    ret = lax.all_to_all(back, "expert", split_axis=1, concat_axis=1, tiled=True)
    ret = ret.reshape(experts * capacity, -1)
    ret_rows = ret[:, :model_width].astype(jnp.float32)
    ret_gate = jnp.sum(
        ret[:, model_width : model_width + 2 * copies].astype(jnp.float32), axis=1
    )
    grad_w_in = grad_in[None]
    grad_w_out = grad_out[None]
    mixed_grad = jnp.dot(assign, ret_rows, precision=PRECISE)
    gate_grads = jnp.einsum("tks,s->tk", spread, ret_gate, precision=PRECISE)
    logit_grad = first_gate * second_gate * (gate_grads[:, 0] - gate_grads[:, 1])
    logits_grad = logit_grad[:, None] * (chosen[:, 0] - chosen[:, 1])
    normed_grad = mixed_grad + lax.dot_general(
        logits_grad, router_weight, (((1,), (1,)), ((), ())), precision=PRECISE
    )
    local_router = lax.dot_general(
        normed_in.astype(jnp.float32), logits_grad, (((0,), (0,)), ((), ())), precision=PRECISE
    )
    local_gain = jnp.sum(normed_grad * normed, axis=0)
    local_bias = jnp.sum(normed_grad, axis=0)
    summed = all_sum(
        jnp.concatenate([local_router, local_gain[:, None], local_bias[:, None]], axis=1)
    )
    grad_router = summed[:, :experts]
    grad_gain = summed[:, experts]
    grad_bias = summed[:, experts + 1]
    scaled = normed_grad * norm_gain
    branch = inverse * (
        scaled
        - jnp.mean(scaled, axis=1, keepdims=True)
        - normed * jnp.mean(scaled * normed, axis=1, keepdims=True)
    )
    grad_tokens = (grad_kept.astype(jnp.float32) + branch).astype(jnp.bfloat16)
    return (grad_tokens, grad_w_in, grad_w_out, grad_router, grad_gain, grad_bias)


def solution(mesh):
    placed = (
        P(("expert", "rep"), None),
        P(("expert", "rep"), None, None),
        P(("expert", "rep"), None),
        P(("expert", "rep"), None),
        P(),
        P(),
        P(),
        P("expert", None, "rep"),
        P("expert", "rep", None),
    )
    return jax.shard_map(
        on_device,
        mesh=mesh,
        in_specs=placed,
        out_specs=(
            P(("expert", "rep"), None),
            P("expert", None, "rep"),
            P("expert", "rep", None),
            P(),
            P(),
            P(),
        ),
        check_vma=False,
    )
```

```python
import jax
import jax.numpy as jnp
from jax import lax
from jax.sharding import PartitionSpec as P

NORM_EPS = 1e-06
PRECISE = lax.Precision.HIGHEST


def gelu_parts(preact):
    normal_cdf = 0.5 * (1.0 + lax.erf(preact * 0.7071067811865476))
    density = jnp.exp(-0.5 * preact * preact) * 0.3989422804014327
    return (preact * normal_cdf, normal_cdf + preact * density)


def contract(left, right, left_axis, right_axis):
    return lax.dot_general(
        left, right, (((left_axis,), (right_axis,)), ((), ())), preferred_element_type=jnp.float32
    )


def layer_norm(tokens, norm_gain, norm_bias):
    values = tokens.astype(jnp.float32)
    center = values - jnp.mean(values, axis=1, keepdims=True)
    inverse = 1.0 / jnp.sqrt(jnp.mean(center * center, axis=1, keepdims=True) + NORM_EPS)
    normed = center * inverse
    return (normed, inverse, (normed * norm_gain + norm_bias).astype(jnp.bfloat16))


def gate_values(normed_in, router_weight, expert_ids):
    experts = router_weight.shape[1]
    logits = jnp.dot(normed_in.astype(jnp.float32), router_weight, precision=PRECISE)
    chosen = (expert_ids[:, :, None] == jnp.arange(experts, dtype=jnp.int32)[None, None, :]).astype(
        jnp.float32
    )
    picked = jnp.sum(logits[:, None, :] * chosen, axis=2)
    first_gate = jax.nn.sigmoid(picked[:, 0] - picked[:, 1])
    second_gate = jax.nn.sigmoid(picked[:, 1] - picked[:, 0])
    return (chosen, first_gate, second_gate)


def expert_rows(normed_rows, grad_rows, gate_rows, weight_in, weight_out):
    preact = contract(normed_rows, weight_in, 1, 0)
    hidden, hidden_slope = gelu_parts(preact)
    gate_col = gate_rows.astype(jnp.float32)[:, None]
    weighted = (gate_col * hidden).astype(jnp.bfloat16)
    back_hidden = contract(grad_rows, weight_out, 1, 1)
    gate_grad = jnp.sum(back_hidden * hidden, axis=1)
    pre_grad = (gate_col * back_hidden * hidden_slope).astype(jnp.bfloat16)
    grad_out = contract(weighted, grad_rows, 0, 0)
    grad_in = contract(normed_rows, pre_grad, 0, 0)
    input_grad = contract(pre_grad, weight_in, 1, 1)
    return (input_grad, gate_grad, grad_in, grad_out)


def all_sum(part):
    devices = lax.axis_size("expert") * lax.axis_size("rep")
    flat = part.reshape(-1)
    width = -(-flat.shape[0] // (devices * 128)) * 128
    flat = jnp.pad(flat, (0, devices * width - flat.shape[0]))
    pieces = lax.all_to_all(
        flat.reshape(devices, width), ("expert", "rep"), split_axis=0, concat_axis=0, tiled=True
    )
    mine = jnp.sum(pieces, axis=0)
    spread_out = jnp.broadcast_to(mine[None], (devices, width))
    whole = lax.all_to_all(spread_out, ("expert", "rep"), split_axis=0, concat_axis=0, tiled=True)
    return whole.reshape(-1)[: part.size].reshape(part.shape)


def on_device(
    tokens, grad_grid, keep_order, expert_ids, norm_gain, norm_bias, router_weight, w_in, w_out
):
    experts = router_weight.shape[1]
    tok_count = tokens.shape[0]
    model_width = tokens.shape[1]
    capacity = 5 * tok_count // (2 * experts)
    kept_count = tok_count // grad_grid.shape[0]
    lane = 128
    grad_kept = jnp.take_along_axis(grad_grid, keep_order[:, :kept_count, None], axis=1).reshape(
        tok_count, model_width
    )
    normed, inverse, normed_in = layer_norm(tokens, norm_gain, norm_bias)
    chosen, first_gate, second_gate = gate_values(normed_in, router_weight, expert_ids)
    gate_half = jnp.stack([first_gate, second_gate], axis=1).astype(jnp.bfloat16)
    expert_hits = jnp.sum(chosen, axis=1)
    before = jnp.cumsum(expert_hits, axis=0) - expert_hits
    slot_place = jnp.sum(before[:, None, :] * chosen, axis=2).astype(jnp.int32)
    slot_index = slot_place * experts + expert_ids
    slot_ids = jnp.arange(experts * capacity, dtype=jnp.int32)
    spread = (slot_index[:, :, None] == slot_ids[None, None, :]).astype(jnp.float32)
    assign = jnp.sum(spread, axis=1)
    assign_half = assign.astype(jnp.bfloat16)
    both = jnp.concatenate([normed_in, grad_kept], axis=1)
    send_rows = contract(assign_half, both, 0, 0).astype(jnp.bfloat16)
    send_gate = jnp.einsum(
        "tks,tk->s", spread, gate_half.astype(jnp.float32), precision=PRECISE
    ).astype(jnp.bfloat16)
    gate_block = jnp.concatenate(
        [send_gate[:, None], jnp.zeros((experts * capacity, lane - 1), jnp.bfloat16)], axis=1
    )
    send = jnp.concatenate([send_rows, gate_block], axis=1).reshape(capacity, experts, -1)
    rep_at = lax.axis_index("rep")
    copies = lax.axis_size("rep")
    cols = jnp.arange(lane, dtype=jnp.int32)[None, :]
    zero = jnp.zeros((), jnp.bfloat16)
    half = capacity // 2
    bounds = ((0, half), (half, capacity))
    ret_parts, in_parts, out_parts = ([], [], [])
    for low, high in bounds:
        got = lax.all_to_all(send[low:high], "expert", split_axis=1, concat_axis=1, tiled=True)
        got = lax.all_gather(got, "rep", axis=0, tiled=False)
        got = got.reshape(-1, got.shape[-1])
        input_grad, gate_grad, grad_in, grad_out = expert_rows(
            got[:, :model_width],
            got[:, model_width : 2 * model_width],
            got[:, 2 * model_width],
            w_in[0],
            w_out[0],
        )
        in_parts.append(grad_in)
        out_parts.append(grad_out)
        rows_here = input_grad.shape[0]
        gate_hi = gate_grad.astype(jnp.bfloat16)
        gate_lo = (gate_grad - gate_hi.astype(jnp.float32)).astype(jnp.bfloat16)
        gate_cols = jnp.where(
            cols == 2 * rep_at,
            gate_hi[:, None],
            jnp.where(cols == 2 * rep_at + 1, gate_lo[:, None], zero),
        )
        packed = jnp.concatenate([input_grad.astype(jnp.bfloat16), gate_cols], axis=1)
        packed = packed.reshape(copies, rows_here // copies, -1)
        back = lax.psum_scatter(packed, "rep", scatter_dimension=0, tiled=True)
        back = back.reshape(high - low, experts, -1)
        ret_parts.append(
            lax.all_to_all(back, "expert", split_axis=1, concat_axis=1, tiled=True)
        )
    ret = jnp.concatenate(ret_parts, axis=0).reshape(experts * capacity, -1)
    ret_rows = ret[:, :model_width].astype(jnp.float32)
    ret_gate = jnp.sum(
        ret[:, model_width : model_width + 2 * copies].astype(jnp.float32), axis=1
    )
    grad_in = in_parts[0] + in_parts[1]
    grad_out = out_parts[0] + out_parts[1]
    grad_w_in = grad_in[None]
    grad_w_out = grad_out[None]
    mixed_grad = jnp.dot(assign, ret_rows, precision=PRECISE)
    gate_grads = jnp.einsum("tks,s->tk", spread, ret_gate, precision=PRECISE)
    logit_grad = first_gate * second_gate * (gate_grads[:, 0] - gate_grads[:, 1])
    logits_grad = logit_grad[:, None] * (chosen[:, 0] - chosen[:, 1])
    normed_grad = mixed_grad + lax.dot_general(
        logits_grad, router_weight, (((1,), (1,)), ((), ())), precision=PRECISE
    )
    local_router = lax.dot_general(
        normed_in.astype(jnp.float32), logits_grad, (((0,), (0,)), ((), ())), precision=PRECISE
    )
    local_gain = jnp.sum(normed_grad * normed, axis=0)
    local_bias = jnp.sum(normed_grad, axis=0)
    summed = all_sum(
        jnp.concatenate([local_router, local_gain[:, None], local_bias[:, None]], axis=1)
    )
    grad_router = summed[:, :experts]
    grad_gain = summed[:, experts]
    grad_bias = summed[:, experts + 1]
    scaled = normed_grad * norm_gain
    branch = inverse * (
        scaled
        - jnp.mean(scaled, axis=1, keepdims=True)
        - normed * jnp.mean(scaled * normed, axis=1, keepdims=True)
    )
    grad_tokens = (grad_kept.astype(jnp.float32) + branch).astype(jnp.bfloat16)
    return (grad_tokens, grad_w_in, grad_w_out, grad_router, grad_gain, grad_bias)


def solution(mesh):
    placed = (
        P(("expert", "rep"), None),
        P(("expert", "rep"), None, None),
        P(("expert", "rep"), None),
        P(("expert", "rep"), None),
        P(),
        P(),
        P(),
        P("expert", None, "rep"),
        P("expert", "rep", None),
    )
    return jax.shard_map(
        on_device,
        mesh=mesh,
        in_specs=placed,
        out_specs=(
            P(("expert", "rep"), None),
            P("expert", None, "rep"),
            P("expert", "rep", None),
            P(),
            P(),
            P(),
        ),
        check_vma=False,
    )
```

```python
import jax
import jax.numpy as jnp
from jax import lax
from jax.sharding import PartitionSpec as P

NORM_EPS = 1e-06
PRECISE = lax.Precision.HIGHEST


def gelu_parts(preact):
    normal_cdf = 0.5 * (1.0 + lax.erf(preact * 0.7071067811865476))
    density = jnp.exp(-0.5 * preact * preact) * 0.3989422804014327
    return (preact * normal_cdf, normal_cdf + preact * density)


def contract(left, right, left_axis, right_axis):
    return lax.dot_general(
        left, right, (((left_axis,), (right_axis,)), ((), ())), preferred_element_type=jnp.float32
    )


def layer_norm(tokens, norm_gain, norm_bias):
    values = tokens.astype(jnp.float32)
    center = values - jnp.mean(values, axis=1, keepdims=True)
    inverse = 1.0 / jnp.sqrt(jnp.mean(center * center, axis=1, keepdims=True) + NORM_EPS)
    normed = center * inverse
    return (normed, inverse, (normed * norm_gain + norm_bias).astype(jnp.bfloat16))


def gate_values(normed_in, router_weight, expert_ids):
    experts = router_weight.shape[1]
    logits = jnp.dot(normed_in.astype(jnp.float32), router_weight, precision=PRECISE)
    chosen = (expert_ids[:, :, None] == jnp.arange(experts, dtype=jnp.int32)[None, None, :]).astype(
        jnp.float32
    )
    picked = jnp.sum(logits[:, None, :] * chosen, axis=2)
    first_gate = jax.nn.sigmoid(picked[:, 0] - picked[:, 1])
    second_gate = jax.nn.sigmoid(picked[:, 1] - picked[:, 0])
    return (chosen, first_gate, second_gate)


def expert_rows(normed_rows, grad_rows, gate_rows, weight_in, weight_out):
    preact = contract(normed_rows, weight_in, 1, 0)
    hidden, hidden_slope = gelu_parts(preact)
    gate_col = gate_rows.astype(jnp.float32)[:, None]
    weighted = (gate_col * hidden).astype(jnp.bfloat16)
    back_hidden = contract(grad_rows, weight_out, 1, 1)
    gate_grad = jnp.sum(back_hidden * hidden, axis=1)
    pre_grad = (gate_col * back_hidden * hidden_slope).astype(jnp.bfloat16)
    grad_out = contract(weighted, grad_rows, 0, 0)
    grad_in = contract(normed_rows, pre_grad, 0, 0)
    input_grad = contract(pre_grad, weight_in, 1, 1)
    return (input_grad, gate_grad, grad_in, grad_out)


def all_sum(part):
    devices = lax.axis_size("expert") * lax.axis_size("rep")
    flat = part.reshape(-1)
    width = -(-flat.shape[0] // (devices * 128)) * 128
    flat = jnp.pad(flat, (0, devices * width - flat.shape[0]))
    pieces = lax.all_to_all(
        flat.reshape(devices, width), ("expert", "rep"), split_axis=0, concat_axis=0, tiled=True
    )
    mine = jnp.sum(pieces, axis=0)
    spread_out = jnp.broadcast_to(mine[None], (devices, width))
    whole = lax.all_to_all(spread_out, ("expert", "rep"), split_axis=0, concat_axis=0, tiled=True)
    return whole.reshape(-1)[: part.size].reshape(part.shape)


def layer_body(
    tokens, grad_grid, keep_order, expert_ids, norm_gain, norm_bias, router_weight, w_in, w_out
):
    experts = router_weight.shape[1]
    tok_count = tokens.shape[0]
    model_width = tokens.shape[1]
    capacity = 5 * tok_count // (2 * experts)
    kept_count = tok_count // grad_grid.shape[0]
    lane = 128
    grad_kept = jnp.take_along_axis(grad_grid, keep_order[:, :kept_count, None], axis=1).reshape(
        tok_count, model_width
    )
    normed, inverse, normed_in = layer_norm(tokens, norm_gain, norm_bias)
    chosen, first_gate, second_gate = gate_values(normed_in, router_weight, expert_ids)
    gate_half = jnp.stack([first_gate, second_gate], axis=1).astype(jnp.bfloat16)
    expert_hits = jnp.sum(chosen, axis=1)
    before = jnp.cumsum(expert_hits, axis=0) - expert_hits
    slot_place = jnp.sum(before[:, None, :] * chosen, axis=2).astype(jnp.int32)
    slot_index = slot_place * experts + expert_ids
    slot_ids = jnp.arange(experts * capacity, dtype=jnp.int32)
    spread = (slot_index[:, :, None] == slot_ids[None, None, :]).astype(jnp.float32)
    assign = jnp.sum(spread, axis=1)
    assign_half = assign.astype(jnp.bfloat16)
    both = jnp.concatenate([normed_in, grad_kept], axis=1)
    send_rows = contract(assign_half, both, 0, 0).astype(jnp.bfloat16)
    send_gate = jnp.einsum(
        "tks,tk->s", spread, gate_half.astype(jnp.float32), precision=PRECISE
    ).astype(jnp.bfloat16)
    gate_block = jnp.concatenate(
        [send_gate[:, None], jnp.zeros((experts * capacity, lane - 1), jnp.bfloat16)], axis=1
    )
    send = jnp.concatenate([send_rows, gate_block], axis=1).reshape(capacity, experts, -1)
    rep_at = lax.axis_index("rep")
    copies = lax.axis_size("rep")
    cols = jnp.arange(lane, dtype=jnp.int32)[None, :]
    zero = jnp.zeros((), jnp.bfloat16)
    is_hi = cols == 2 * rep_at
    is_lo = cols == 2 * rep_at + 1
    half = capacity // 2
    bounds = ((0, half), (half, capacity))
    ret_parts, in_parts, out_parts = ([], [], [])
    for chunk, (low, high) in enumerate(bounds):
        if chunk == 0:
            got = lax.all_to_all(send[low:high], "expert", split_axis=1, concat_axis=1, tiled=True)
            got = lax.all_gather(got, "rep", axis=0, tiled=False)
        else:
            part = send[low:high]
            wide = jnp.broadcast_to(
                part[:, :, None], (high - low, experts, copies, part.shape[-1])
            ).reshape(high - low, experts * copies, -1)
            got = lax.all_to_all(wide, ("expert", "rep"), split_axis=1, concat_axis=1, tiled=True)
            got = got.reshape(high - low, experts, copies, -1).transpose(2, 0, 1, 3)
        got = got.reshape(-1, got.shape[-1])
        weight_in, weight_out, at_hi, at_lo = (w_in[0], w_out[0], is_hi, is_lo)
        if chunk:
            weight_in, weight_out, at_hi, at_lo = lax.optimization_barrier(
                (weight_in, weight_out, at_hi, at_lo)
            )
        input_grad, gate_grad, grad_in, grad_out = expert_rows(
            got[:, :model_width],
            got[:, model_width : 2 * model_width],
            got[:, 2 * model_width],
            weight_in,
            weight_out,
        )
        in_parts.append(grad_in)
        out_parts.append(grad_out)
        rows_here = input_grad.shape[0]
        gate_hi = gate_grad.astype(jnp.bfloat16)
        gate_lo = (gate_grad - gate_hi.astype(jnp.float32)).astype(jnp.bfloat16)
        gate_cols = jnp.where(at_hi, gate_hi[:, None], jnp.where(at_lo, gate_lo[:, None], zero))
        packed = jnp.concatenate([input_grad.astype(jnp.bfloat16), gate_cols], axis=1)
        packed = packed.reshape(copies, rows_here // copies, -1)
        back = lax.psum_scatter(packed, "rep", scatter_dimension=0, tiled=True)
        back = back.reshape(high - low, experts, -1)
        ret_parts.append(lax.all_to_all(back, "expert", split_axis=1, concat_axis=1, tiled=True))
    ret = jnp.concatenate(ret_parts, axis=0).reshape(experts * capacity, -1)
    ret_rows = ret[:, :model_width].astype(jnp.float32)
    ret_gate = jnp.sum(
        ret[:, model_width : model_width + 2 * copies].astype(jnp.float32), axis=1
    )
    grad_in = in_parts[0] + in_parts[1]
    grad_out = out_parts[0] + out_parts[1]
    grad_w_in = grad_in[None]
    grad_w_out = grad_out[None]
    mixed_grad = jnp.dot(assign, ret_rows, precision=PRECISE)
    gate_grads = jnp.einsum("tks,s->tk", spread, ret_gate, precision=PRECISE)
    logit_grad = first_gate * second_gate * (gate_grads[:, 0] - gate_grads[:, 1])
    logits_grad = logit_grad[:, None] * (chosen[:, 0] - chosen[:, 1])
    normed_grad = mixed_grad + lax.dot_general(
        logits_grad, router_weight, (((1,), (1,)), ((), ())), precision=PRECISE
    )
    local_router = lax.dot_general(
        normed_in.astype(jnp.float32), logits_grad, (((0,), (0,)), ((), ())), precision=PRECISE
    )
    local_gain = jnp.sum(normed_grad * normed, axis=0)
    local_bias = jnp.sum(normed_grad, axis=0)
    summed = all_sum(
        jnp.concatenate([local_router, local_gain[:, None], local_bias[:, None]], axis=1)
    )
    grad_router = summed[:, :experts]
    grad_gain = summed[:, experts]
    grad_bias = summed[:, experts + 1]
    scaled = normed_grad * norm_gain
    branch = inverse * (
        scaled
        - jnp.mean(scaled, axis=1, keepdims=True)
        - normed * jnp.mean(scaled * normed, axis=1, keepdims=True)
    )
    grad_tokens = (grad_kept.astype(jnp.float32) + branch).astype(jnp.bfloat16)
    return (grad_tokens, grad_w_in, grad_w_out, grad_router, grad_gain, grad_bias)


def solution(mesh):
    placed = (
        P(("expert", "rep"), None),
        P(("expert", "rep"), None, None),
        P(("expert", "rep"), None),
        P(("expert", "rep"), None),
        P(),
        P(),
        P(),
        P("expert", None, "rep"),
        P("expert", "rep", None),
    )
    return jax.shard_map(
        layer_body,
        mesh=mesh,
        in_specs=placed,
        out_specs=(
            P(("expert", "rep"), None),
            P("expert", None, "rep"),
            P("expert", "rep", None),
            P(),
            P(),
            P(),
        ),
        check_vma=False,
    )
```

```python
import jax
import jax.numpy as jnp
from jax import lax
from jax.sharding import PartitionSpec as P

NORM_EPS = 1e-06
PRECISE = lax.Precision.HIGHEST


def gelu_parts(preact):
    normal_cdf = 0.5 * (1.0 + lax.erf(preact * 0.7071067811865476))
    density = jnp.exp(-0.5 * preact * preact) * 0.3989422804014327
    return (preact * normal_cdf, normal_cdf + preact * density)


def contract(left, right, left_axis, right_axis):
    return lax.dot_general(
        left, right, (((left_axis,), (right_axis,)), ((), ())), preferred_element_type=jnp.float32
    )


def layer_norm(tokens, norm_gain, norm_bias):
    values = tokens.astype(jnp.float32)
    center = values - jnp.mean(values, axis=1, keepdims=True)
    inverse = 1.0 / jnp.sqrt(jnp.mean(center * center, axis=1, keepdims=True) + NORM_EPS)
    normed = center * inverse
    return (normed, inverse, (normed * norm_gain + norm_bias).astype(jnp.bfloat16))


def gate_values(normed_in, router_weight, expert_ids):
    experts = router_weight.shape[1]
    logits = jnp.dot(normed_in.astype(jnp.float32), router_weight, precision=PRECISE)
    chosen = (expert_ids[:, :, None] == jnp.arange(experts, dtype=jnp.int32)[None, None, :]).astype(
        jnp.float32
    )
    picked = jnp.sum(logits[:, None, :] * chosen, axis=2)
    first_gate = jax.nn.sigmoid(picked[:, 0] - picked[:, 1])
    second_gate = jax.nn.sigmoid(picked[:, 1] - picked[:, 0])
    return (chosen, first_gate, second_gate)


def expert_rows(normed_rows, grad_rows, gate_rows, weight_in, weight_out):
    preact = contract(normed_rows, weight_in, 1, 0)
    hidden, hidden_slope = gelu_parts(preact)
    gate_col = gate_rows.astype(jnp.float32)[:, None]
    weighted = (gate_col * hidden).astype(jnp.bfloat16)
    back_hidden = contract(grad_rows, weight_out, 1, 1)
    gate_grad = jnp.sum(back_hidden * hidden, axis=1)
    pre_grad = (gate_col * back_hidden * hidden_slope).astype(jnp.bfloat16)
    grad_out = contract(weighted, grad_rows, 0, 0)
    grad_in = contract(normed_rows, pre_grad, 0, 0)
    input_grad = contract(pre_grad, weight_in, 1, 1)
    return (input_grad, gate_grad, grad_in, grad_out)


def all_sum(part):
    devices = lax.axis_size("expert") * lax.axis_size("rep")
    flat = part.reshape(-1)
    width = -(-flat.shape[0] // (devices * 128)) * 128
    flat = jnp.pad(flat, (0, devices * width - flat.shape[0]))
    pieces = lax.all_to_all(
        flat.reshape(devices, width), ("expert", "rep"), split_axis=0, concat_axis=0, tiled=True
    )
    mine = jnp.sum(pieces, axis=0)
    spread_out = jnp.broadcast_to(mine[None], (devices, width))
    whole = lax.all_to_all(spread_out, ("expert", "rep"), split_axis=0, concat_axis=0, tiled=True)
    return whole.reshape(-1)[: part.size].reshape(part.shape)


def layer_body(
    tokens, grad_grid, keep_order, expert_ids, norm_gain, norm_bias, router_weight, w_in, w_out
):
    experts = router_weight.shape[1]
    tok_count = tokens.shape[0]
    model_width = tokens.shape[1]
    capacity = 5 * tok_count // (2 * experts)
    kept_count = tok_count // grad_grid.shape[0]
    lane = 128
    grad_kept = jnp.take_along_axis(grad_grid, keep_order[:, :kept_count, None], axis=1).reshape(
        tok_count, model_width
    )
    normed, inverse, normed_in = layer_norm(tokens, norm_gain, norm_bias)
    chosen, first_gate, second_gate = gate_values(normed_in, router_weight, expert_ids)
    gate_half = jnp.stack([first_gate, second_gate], axis=1).astype(jnp.bfloat16)
    expert_hits = jnp.sum(chosen, axis=1)
    before = jnp.cumsum(expert_hits, axis=0) - expert_hits
    slot_place = jnp.sum(before[:, None, :] * chosen, axis=2).astype(jnp.int32)
    slot_index = slot_place * experts + expert_ids
    slot_ids = jnp.arange(experts * capacity, dtype=jnp.int32)
    spread = (slot_index[:, :, None] == slot_ids[None, None, :]).astype(jnp.float32)
    assign = jnp.sum(spread, axis=1)
    assign_half = assign.astype(jnp.bfloat16)
    both = jnp.concatenate([normed_in, grad_kept], axis=1)
    send_rows = contract(assign_half, both, 0, 0).astype(jnp.bfloat16)
    send_gate = jnp.einsum(
        "tks,tk->s", spread, gate_half.astype(jnp.float32), precision=PRECISE
    ).astype(jnp.bfloat16)
    gate_block = jnp.concatenate(
        [send_gate[:, None], jnp.zeros((experts * capacity, lane - 1), jnp.bfloat16)], axis=1
    )
    send = jnp.concatenate([send_rows, gate_block], axis=1).reshape(capacity, experts, -1)
    rep_at = lax.axis_index("rep")
    copies = lax.axis_size("rep")
    cols = jnp.arange(lane, dtype=jnp.int32)[None, :]
    zero = jnp.zeros((), jnp.bfloat16)
    is_hi = cols == 2 * rep_at
    is_lo = cols == 2 * rep_at + 1
    half = (3 * capacity + 4) // 5
    bounds = ((0, half), (half, capacity))
    ret_parts, in_parts, out_parts = ([], [], [])
    for chunk, (low, high) in enumerate(bounds):
        got = lax.all_to_all(send[low:high], "expert", split_axis=1, concat_axis=1, tiled=True)
        got = lax.all_gather(got, "rep", axis=0, tiled=False)
        got = got.reshape(-1, got.shape[-1])
        weight_in, weight_out, at_hi, at_lo = (w_in[0], w_out[0], is_hi, is_lo)
        if chunk:
            weight_in, weight_out, at_hi, at_lo = lax.optimization_barrier(
                (weight_in, weight_out, at_hi, at_lo)
            )
        input_grad, gate_grad, grad_in, grad_out = expert_rows(
            got[:, :model_width],
            got[:, model_width : 2 * model_width],
            got[:, 2 * model_width],
            weight_in,
            weight_out,
        )
        in_parts.append(grad_in)
        out_parts.append(grad_out)
        rows_here = input_grad.shape[0]
        gate_hi = gate_grad.astype(jnp.bfloat16)
        gate_lo = (gate_grad - gate_hi.astype(jnp.float32)).astype(jnp.bfloat16)
        gate_cols = jnp.where(at_hi, gate_hi[:, None], jnp.where(at_lo, gate_lo[:, None], zero))
        packed = jnp.concatenate([input_grad.astype(jnp.bfloat16), gate_cols], axis=1)
        packed = packed.reshape(copies, rows_here // copies, -1)
        back = lax.psum_scatter(packed, "rep", scatter_dimension=0, tiled=True)
        back = back.reshape(high - low, experts, -1)
        ret_parts.append(lax.all_to_all(back, "expert", split_axis=1, concat_axis=1, tiled=True))
    ret = jnp.concatenate(ret_parts, axis=0).reshape(experts * capacity, -1)
    ret_rows = ret[:, :model_width].astype(jnp.float32)
    ret_gate = jnp.sum(
        ret[:, model_width : model_width + 2 * copies].astype(jnp.float32), axis=1
    )
    grad_in = in_parts[0] + in_parts[1]
    grad_out = out_parts[0] + out_parts[1]
    grad_w_in = grad_in[None]
    grad_w_out = grad_out[None]
    mixed_grad = jnp.dot(assign, ret_rows, precision=PRECISE)
    gate_grads = jnp.einsum("tks,s->tk", spread, ret_gate, precision=PRECISE)
    logit_grad = first_gate * second_gate * (gate_grads[:, 0] - gate_grads[:, 1])
    logits_grad = logit_grad[:, None] * (chosen[:, 0] - chosen[:, 1])
    normed_grad = mixed_grad + lax.dot_general(
        logits_grad, router_weight, (((1,), (1,)), ((), ())), precision=PRECISE
    )
    local_router = lax.dot_general(
        normed_in.astype(jnp.float32), logits_grad, (((0,), (0,)), ((), ())), precision=PRECISE
    )
    local_gain = jnp.sum(normed_grad * normed, axis=0)
    local_bias = jnp.sum(normed_grad, axis=0)
    summed = all_sum(
        jnp.concatenate([local_router, local_gain[:, None], local_bias[:, None]], axis=1)
    )
    grad_router = summed[:, :experts]
    grad_gain = summed[:, experts]
    grad_bias = summed[:, experts + 1]
    scaled = normed_grad * norm_gain
    branch = inverse * (
        scaled
        - jnp.mean(scaled, axis=1, keepdims=True)
        - normed * jnp.mean(scaled * normed, axis=1, keepdims=True)
    )
    grad_tokens = (grad_kept.astype(jnp.float32) + branch).astype(jnp.bfloat16)
    return (grad_tokens, grad_w_in, grad_w_out, grad_router, grad_gain, grad_bias)


def solution(mesh):
    placed = (
        P(("expert", "rep"), None),
        P(("expert", "rep"), None, None),
        P(("expert", "rep"), None),
        P(("expert", "rep"), None),
        P(),
        P(),
        P(),
        P("expert", None, "rep"),
        P("expert", "rep", None),
    )
    return jax.shard_map(
        layer_body,
        mesh=mesh,
        in_specs=placed,
        out_specs=(
            P(("expert", "rep"), None),
            P("expert", None, "rep"),
            P("expert", "rep", None),
            P(),
            P(),
            P(),
        ),
        check_vma=False,
    )
```

```python
import jax
import jax.numpy as jnp
from jax import lax
from jax.sharding import PartitionSpec as P

NORM_EPS = 1e-06
PRECISE = lax.Precision.HIGHEST


def gelu_parts(preact):
    normal_cdf = 0.5 * (1.0 + lax.erf(preact * 0.7071067811865476))
    density = jnp.exp(-0.5 * preact * preact) * 0.3989422804014327
    return (preact * normal_cdf, normal_cdf + preact * density)


def contract(left, right, left_axis, right_axis):
    return lax.dot_general(
        left, right, (((left_axis,), (right_axis,)), ((), ())), preferred_element_type=jnp.float32
    )


def layer_norm(tokens, norm_gain, norm_bias):
    values = tokens.astype(jnp.float32)
    center = values - jnp.mean(values, axis=1, keepdims=True)
    inverse = 1.0 / jnp.sqrt(jnp.mean(center * center, axis=1, keepdims=True) + NORM_EPS)
    normed = center * inverse
    return (normed, inverse, (normed * norm_gain + norm_bias).astype(jnp.bfloat16))


def gate_values(normed_in, router_weight, expert_ids):
    experts = router_weight.shape[1]
    logits = jnp.dot(normed_in.astype(jnp.float32), router_weight, precision=PRECISE)
    chosen = (expert_ids[:, :, None] == jnp.arange(experts, dtype=jnp.int32)[None, None, :]).astype(
        jnp.float32
    )
    picked = jnp.sum(logits[:, None, :] * chosen, axis=2)
    first_gate = jax.nn.sigmoid(picked[:, 0] - picked[:, 1])
    second_gate = jax.nn.sigmoid(picked[:, 1] - picked[:, 0])
    return (chosen, first_gate, second_gate)


def expert_rows(normed_rows, grad_rows, gate_rows, weight_in, weight_out):
    preact = contract(normed_rows, weight_in, 1, 0)
    hidden, hidden_slope = gelu_parts(preact)
    gate_col = gate_rows.astype(jnp.float32)[:, None]
    weighted = (gate_col * hidden).astype(jnp.bfloat16)
    back_hidden = contract(grad_rows, weight_out, 1, 1)
    gate_grad = jnp.sum(back_hidden * hidden, axis=1)
    pre_grad = (gate_col * back_hidden * hidden_slope).astype(jnp.bfloat16)
    grad_out = contract(weighted, grad_rows, 0, 0)
    grad_in = contract(normed_rows, pre_grad, 0, 0)
    input_grad = contract(pre_grad, weight_in, 1, 1)
    return (input_grad, gate_grad, grad_in, grad_out)


def all_sum(part):
    devices = lax.axis_size("expert") * lax.axis_size("rep")
    flat = part.reshape(-1)
    width = -(-flat.shape[0] // (devices * 128)) * 128
    flat = jnp.pad(flat, (0, devices * width - flat.shape[0]))
    pieces = lax.all_to_all(
        flat.reshape(devices, width), ("expert", "rep"), split_axis=0, concat_axis=0, tiled=True
    )
    mine = jnp.sum(pieces, axis=0)
    spread_out = jnp.broadcast_to(mine[None], (devices, width))
    whole = lax.all_to_all(spread_out, ("expert", "rep"), split_axis=0, concat_axis=0, tiled=True)
    return whole.reshape(-1)[: part.size].reshape(part.shape)


def layer_body(
    tokens, grad_grid, keep_order, expert_ids, norm_gain, norm_bias, router_weight, w_in, w_out
):
    experts = router_weight.shape[1]
    tok_count = tokens.shape[0]
    model_width = tokens.shape[1]
    capacity = 5 * tok_count // (2 * experts)
    kept_count = tok_count // grad_grid.shape[0]
    lane = 128
    grad_kept = jnp.take_along_axis(grad_grid, keep_order[:, :kept_count, None], axis=1).reshape(
        tok_count, model_width
    )
    normed, inverse, normed_in = layer_norm(tokens, norm_gain, norm_bias)
    chosen, first_gate, second_gate = gate_values(normed_in, router_weight, expert_ids)
    gate_half = jnp.stack([first_gate, second_gate], axis=1).astype(jnp.bfloat16)
    expert_hits = jnp.sum(chosen, axis=1)
    before = jnp.cumsum(expert_hits, axis=0) - expert_hits
    slot_place = jnp.sum(before[:, None, :] * chosen, axis=2).astype(jnp.int32)
    slot_index = slot_place * experts + expert_ids
    slot_ids = jnp.arange(experts * capacity, dtype=jnp.int32)
    spread = (slot_index[:, :, None] == slot_ids[None, None, :]).astype(jnp.float32)
    assign = jnp.sum(spread, axis=1)
    assign_half = assign.astype(jnp.bfloat16)
    both = jnp.concatenate([normed_in, grad_kept], axis=1)
    send_gate = jnp.einsum(
        "tks,tk->s", spread, gate_half.astype(jnp.float32), precision=PRECISE
    ).astype(jnp.bfloat16)

    def send_part(low, high):
        rows = contract(assign_half[:, low * experts : high * experts], both, 0, 0)
        part_gate = send_gate[low * experts : high * experts]
        gate_block = jnp.concatenate(
            [part_gate[:, None], jnp.zeros((part_gate.shape[0], lane - 1), jnp.bfloat16)],
            axis=1,
        )
        whole = jnp.concatenate([rows.astype(jnp.bfloat16), gate_block], axis=1)
        return whole.reshape(high - low, experts, -1)

    rep_at = lax.axis_index("rep")
    copies = lax.axis_size("rep")
    cols = jnp.arange(lane, dtype=jnp.int32)[None, :]
    zero = jnp.zeros((), jnp.bfloat16)
    is_hi = cols == 2 * rep_at
    is_lo = cols == 2 * rep_at + 1
    half = capacity // 2
    bounds = ((0, half), (half, capacity))
    ret_parts, in_parts, out_parts = ([], [], [])
    for chunk, (low, high) in enumerate(bounds):
        got = lax.all_to_all(
            send_part(low, high), "expert", split_axis=1, concat_axis=1, tiled=True
        )
        got = lax.all_gather(got, "rep", axis=0, tiled=False)
        got = got.reshape(-1, got.shape[-1])
        weight_in, weight_out, at_hi, at_lo = (w_in[0], w_out[0], is_hi, is_lo)
        if chunk:
            weight_in, weight_out, at_hi, at_lo = lax.optimization_barrier(
                (weight_in, weight_out, at_hi, at_lo)
            )
        input_grad, gate_grad, grad_in, grad_out = expert_rows(
            got[:, :model_width],
            got[:, model_width : 2 * model_width],
            got[:, 2 * model_width],
            weight_in,
            weight_out,
        )
        in_parts.append(grad_in)
        out_parts.append(grad_out)
        rows_here = input_grad.shape[0]
        gate_hi = gate_grad.astype(jnp.bfloat16)
        gate_lo = (gate_grad - gate_hi.astype(jnp.float32)).astype(jnp.bfloat16)
        gate_cols = jnp.where(at_hi, gate_hi[:, None], jnp.where(at_lo, gate_lo[:, None], zero))
        packed = jnp.concatenate([input_grad.astype(jnp.bfloat16), gate_cols], axis=1)
        packed = packed.reshape(copies, rows_here // copies, -1)
        back = lax.psum_scatter(packed, "rep", scatter_dimension=0, tiled=True)
        back = back.reshape(high - low, experts, -1)
        ret_parts.append(lax.all_to_all(back, "expert", split_axis=1, concat_axis=1, tiled=True))
    ret = jnp.concatenate(ret_parts, axis=0).reshape(experts * capacity, -1)
    ret_rows = ret[:, :model_width].astype(jnp.float32)
    ret_gate = jnp.sum(
        ret[:, model_width : model_width + 2 * copies].astype(jnp.float32), axis=1
    )
    grad_in = in_parts[0] + in_parts[1]
    grad_out = out_parts[0] + out_parts[1]
    grad_w_in = grad_in[None]
    grad_w_out = grad_out[None]
    mixed_grad = jnp.dot(assign, ret_rows, precision=PRECISE)
    gate_grads = jnp.einsum("tks,s->tk", spread, ret_gate, precision=PRECISE)
    logit_grad = first_gate * second_gate * (gate_grads[:, 0] - gate_grads[:, 1])
    logits_grad = logit_grad[:, None] * (chosen[:, 0] - chosen[:, 1])
    normed_grad = mixed_grad + lax.dot_general(
        logits_grad, router_weight, (((1,), (1,)), ((), ())), precision=PRECISE
    )
    local_router = lax.dot_general(
        normed_in.astype(jnp.float32), logits_grad, (((0,), (0,)), ((), ())), precision=PRECISE
    )
    local_gain = jnp.sum(normed_grad * normed, axis=0)
    local_bias = jnp.sum(normed_grad, axis=0)
    summed = all_sum(
        jnp.concatenate([local_router, local_gain[:, None], local_bias[:, None]], axis=1)
    )
    grad_router = summed[:, :experts]
    grad_gain = summed[:, experts]
    grad_bias = summed[:, experts + 1]
    scaled = normed_grad * norm_gain
    branch = inverse * (
        scaled
        - jnp.mean(scaled, axis=1, keepdims=True)
        - normed * jnp.mean(scaled * normed, axis=1, keepdims=True)
    )
    grad_tokens = (grad_kept.astype(jnp.float32) + branch).astype(jnp.bfloat16)
    return (grad_tokens, grad_w_in, grad_w_out, grad_router, grad_gain, grad_bias)


def solution(mesh):
    placed = (
        P(("expert", "rep"), None),
        P(("expert", "rep"), None, None),
        P(("expert", "rep"), None),
        P(("expert", "rep"), None),
        P(),
        P(),
        P(),
        P("expert", None, "rep"),
        P("expert", "rep", None),
    )
    return jax.shard_map(
        layer_body,
        mesh=mesh,
        in_specs=placed,
        out_specs=(
            P(("expert", "rep"), None),
            P("expert", None, "rep"),
            P("expert", "rep", None),
            P(),
            P(),
            P(),
        ),
        check_vma=False,
    )
```

```python
import jax
import jax.numpy as jnp
from jax import lax
from jax.sharding import PartitionSpec as P

NORM_EPS = 1e-06
PRECISE = lax.Precision.HIGHEST


def gelu_parts(preact):
    normal_cdf = 0.5 * (1.0 + lax.erf(preact * 0.7071067811865476))
    density = jnp.exp(-0.5 * preact * preact) * 0.3989422804014327
    return (preact * normal_cdf, normal_cdf + preact * density)


def contract(left, right, left_axis, right_axis):
    return lax.dot_general(
        left, right, (((left_axis,), (right_axis,)), ((), ())), preferred_element_type=jnp.float32
    )


def layer_norm(tokens, norm_gain, norm_bias):
    values = tokens.astype(jnp.float32)
    center = values - jnp.mean(values, axis=1, keepdims=True)
    inverse = 1.0 / jnp.sqrt(jnp.mean(center * center, axis=1, keepdims=True) + NORM_EPS)
    normed = center * inverse
    return (normed, inverse, (normed * norm_gain + norm_bias).astype(jnp.bfloat16))


def gate_values(normed_in, router_weight, expert_ids):
    experts = router_weight.shape[1]
    logits = jnp.dot(normed_in.astype(jnp.float32), router_weight, precision=PRECISE)
    chosen = (expert_ids[:, :, None] == jnp.arange(experts, dtype=jnp.int32)[None, None, :]).astype(
        jnp.float32
    )
    picked = jnp.sum(logits[:, None, :] * chosen, axis=2)
    first_gate = jax.nn.sigmoid(picked[:, 0] - picked[:, 1])
    second_gate = jax.nn.sigmoid(picked[:, 1] - picked[:, 0])
    return (chosen, first_gate, second_gate)


def expert_rows(normed_rows, grad_rows, gate_rows, weight_in, weight_out):
    preact = contract(normed_rows, weight_in, 1, 0)
    hidden, hidden_slope = gelu_parts(preact)
    gate_col = gate_rows.astype(jnp.float32)[:, None]
    weighted = (gate_col * hidden).astype(jnp.bfloat16)
    back_hidden = contract(grad_rows, weight_out, 1, 1)
    gate_grad = jnp.sum(back_hidden * hidden, axis=1)
    pre_grad = (gate_col * back_hidden * hidden_slope).astype(jnp.bfloat16)
    grad_out = contract(weighted, grad_rows, 0, 0)
    grad_in = contract(normed_rows, pre_grad, 0, 0)
    input_grad = contract(pre_grad, weight_in, 1, 1)
    return (input_grad, gate_grad, grad_in, grad_out)


def all_sum(part):
    devices = lax.axis_size("expert") * lax.axis_size("rep")
    flat = part.reshape(-1)
    width = -(-flat.shape[0] // (devices * 128)) * 128
    flat = jnp.pad(flat, (0, devices * width - flat.shape[0]))
    pieces = lax.all_to_all(
        flat.reshape(devices, width), ("expert", "rep"), split_axis=0, concat_axis=0, tiled=True
    )
    mine = jnp.sum(pieces, axis=0)
    spread_out = jnp.broadcast_to(mine[None], (devices, width))
    whole = lax.all_to_all(spread_out, ("expert", "rep"), split_axis=0, concat_axis=0, tiled=True)
    return whole.reshape(-1)[: part.size].reshape(part.shape)


def layer_body(
    tokens, grad_grid, keep_order, expert_ids, norm_gain, norm_bias, router_weight, w_in, w_out
):
    experts = router_weight.shape[1]
    tok_count = tokens.shape[0]
    model_width = tokens.shape[1]
    capacity = 5 * tok_count // (2 * experts)
    kept_count = tok_count // grad_grid.shape[0]
    lane = 128
    grad_kept = jnp.take_along_axis(grad_grid, keep_order[:, :kept_count, None], axis=1).reshape(
        tok_count, model_width
    )
    normed, inverse, normed_in = layer_norm(tokens, norm_gain, norm_bias)
    chosen, first_gate, second_gate = gate_values(normed_in, router_weight, expert_ids)
    gate_half = jnp.stack([first_gate, second_gate], axis=1).astype(jnp.bfloat16)
    expert_hits = jnp.sum(chosen, axis=1)
    before = jnp.cumsum(expert_hits, axis=0) - expert_hits
    slot_place = jnp.sum(before[:, None, :] * chosen, axis=2).astype(jnp.int32)
    slot_index = slot_place * experts + expert_ids
    slot_ids = jnp.arange(experts * capacity, dtype=jnp.int32)
    spread = (slot_index[:, :, None] == slot_ids[None, None, :]).astype(jnp.float32)
    assign = jnp.sum(spread, axis=1)
    assign_half = assign.astype(jnp.bfloat16)
    both = jnp.concatenate([normed_in, grad_kept], axis=1)
    send_gate = jnp.einsum(
        "tks,tk->s", spread, gate_half.astype(jnp.float32), precision=PRECISE
    ).astype(jnp.bfloat16)

    def send_part(low, high):
        count = high - low
        pick = assign_half[:, low * experts : high * experts]
        pick = pick.reshape(-1, count, experts).transpose(0, 2, 1).reshape(pick.shape[0], -1)
        rows = contract(pick, both, 0, 0)
        part_gate = send_gate[low * experts : high * experts]
        part_gate = part_gate.reshape(count, experts).T.reshape(-1)
        gate_block = jnp.concatenate(
            [part_gate[:, None], jnp.zeros((part_gate.shape[0], lane - 1), jnp.bfloat16)],
            axis=1,
        )
        whole = jnp.concatenate([rows.astype(jnp.bfloat16), gate_block], axis=1)
        return whole.reshape(experts, -1)

    rep_at = lax.axis_index("rep")
    copies = lax.axis_size("rep")
    cols = jnp.arange(lane, dtype=jnp.int32)[None, :]
    zero = jnp.zeros((), jnp.bfloat16)
    is_hi = cols == 2 * rep_at
    is_lo = cols == 2 * rep_at + 1
    half = capacity // 2
    bounds = ((0, half), (half, capacity))
    ret_parts, in_parts, out_parts = ([], [], [])
    for chunk, (low, high) in enumerate(bounds):
        got = lax.all_to_all(
            send_part(low, high), "expert", split_axis=0, concat_axis=0, tiled=True
        )
        got = got.reshape(experts, high - low, -1).transpose(1, 0, 2)
        got = lax.all_gather(got, "rep", axis=0, tiled=False)
        got = got.reshape(-1, got.shape[-1])
        weight_in, weight_out, at_hi, at_lo = (w_in[0], w_out[0], is_hi, is_lo)
        if chunk:
            weight_in, weight_out, at_hi, at_lo = lax.optimization_barrier(
                (weight_in, weight_out, at_hi, at_lo)
            )
        input_grad, gate_grad, grad_in, grad_out = expert_rows(
            got[:, :model_width],
            got[:, model_width : 2 * model_width],
            got[:, 2 * model_width],
            weight_in,
            weight_out,
        )
        in_parts.append(grad_in)
        out_parts.append(grad_out)
        rows_here = input_grad.shape[0]
        gate_hi = gate_grad.astype(jnp.bfloat16)
        gate_lo = (gate_grad - gate_hi.astype(jnp.float32)).astype(jnp.bfloat16)
        gate_cols = jnp.where(at_hi, gate_hi[:, None], jnp.where(at_lo, gate_lo[:, None], zero))
        packed = jnp.concatenate([input_grad.astype(jnp.bfloat16), gate_cols], axis=1)
        packed = packed.reshape(copies, rows_here // copies, -1)
        back = lax.psum_scatter(packed, "rep", scatter_dimension=0, tiled=True)
        back = back.reshape(high - low, experts, -1)
        ret_parts.append(lax.all_to_all(back, "expert", split_axis=1, concat_axis=1, tiled=True))
    ret = jnp.concatenate(ret_parts, axis=0).reshape(experts * capacity, -1)
    ret_rows = ret[:, :model_width].astype(jnp.float32)
    ret_gate = jnp.sum(
        ret[:, model_width : model_width + 2 * copies].astype(jnp.float32), axis=1
    )
    grad_in = in_parts[0] + in_parts[1]
    grad_out = out_parts[0] + out_parts[1]
    grad_w_in = grad_in[None]
    grad_w_out = grad_out[None]
    mixed_grad = jnp.dot(assign, ret_rows, precision=PRECISE)
    gate_grads = jnp.einsum("tks,s->tk", spread, ret_gate, precision=PRECISE)
    logit_grad = first_gate * second_gate * (gate_grads[:, 0] - gate_grads[:, 1])
    logits_grad = logit_grad[:, None] * (chosen[:, 0] - chosen[:, 1])
    normed_grad = mixed_grad + lax.dot_general(
        logits_grad, router_weight, (((1,), (1,)), ((), ())), precision=PRECISE
    )
    router_t = lax.dot_general(
        logits_grad, normed_in.astype(jnp.float32), (((0,), (0,)), ((), ())), precision=PRECISE
    )
    local_gain = jnp.sum(normed_grad * normed, axis=0)
    local_bias = jnp.sum(normed_grad, axis=0)
    summed = all_sum(jnp.concatenate([router_t.reshape(-1), local_gain, local_bias]))
    router_size = router_t.size
    grad_router = summed[:router_size].reshape(experts, model_width).T
    grad_gain = summed[router_size : router_size + model_width]
    grad_bias = summed[router_size + model_width :]
    scaled = normed_grad * norm_gain
    branch = inverse * (
        scaled
        - jnp.mean(scaled, axis=1, keepdims=True)
        - normed * jnp.mean(scaled * normed, axis=1, keepdims=True)
    )
    grad_tokens = (grad_kept.astype(jnp.float32) + branch).astype(jnp.bfloat16)
    return (grad_tokens, grad_w_in, grad_w_out, grad_router, grad_gain, grad_bias)


def solution(mesh):
    placed = (
        P(("expert", "rep"), None),
        P(("expert", "rep"), None, None),
        P(("expert", "rep"), None),
        P(("expert", "rep"), None),
        P(),
        P(),
        P(),
        P("expert", None, "rep"),
        P("expert", "rep", None),
    )
    return jax.shard_map(
        layer_body,
        mesh=mesh,
        in_specs=placed,
        out_specs=(
            P(("expert", "rep"), None),
            P("expert", None, "rep"),
            P("expert", "rep", None),
            P(),
            P(),
            P(),
        ),
        check_vma=False,
    )
```

```python
import jax
import jax.numpy as jnp
from jax import lax
from jax.sharding import PartitionSpec as P

NORM_EPS = 1e-06
PRECISE = lax.Precision.HIGHEST


def gelu_parts(preact):
    normal_cdf = 0.5 * (1.0 + lax.erf(preact * 0.7071067811865476))
    density = jnp.exp(-0.5 * preact * preact) * 0.3989422804014327
    return (preact * normal_cdf, normal_cdf + preact * density)


def contract(left, right, left_axis, right_axis):
    return lax.dot_general(
        left, right, (((left_axis,), (right_axis,)), ((), ())), preferred_element_type=jnp.float32
    )


def layer_norm(tokens, norm_gain, norm_bias):
    values = tokens.astype(jnp.float32)
    center = values - jnp.mean(values, axis=1, keepdims=True)
    inverse = 1.0 / jnp.sqrt(jnp.mean(center * center, axis=1, keepdims=True) + NORM_EPS)
    normed = center * inverse
    return (normed, inverse, (normed * norm_gain + norm_bias).astype(jnp.bfloat16))


def gate_values(normed_in, router_weight, expert_ids):
    experts = router_weight.shape[1]
    logits = jnp.dot(normed_in.astype(jnp.float32), router_weight, precision=PRECISE)
    chosen = (expert_ids[:, :, None] == jnp.arange(experts, dtype=jnp.int32)[None, None, :]).astype(
        jnp.float32
    )
    picked = jnp.sum(logits[:, None, :] * chosen, axis=2)
    first_gate = jax.nn.sigmoid(picked[:, 0] - picked[:, 1])
    second_gate = jax.nn.sigmoid(picked[:, 1] - picked[:, 0])
    return (chosen, first_gate, second_gate)


def expert_rows(normed_rows, grad_rows, gate_rows, weight_in, weight_out):
    preact = contract(normed_rows, weight_in, 1, 0)
    hidden, hidden_slope = gelu_parts(preact)
    gate_col = gate_rows.astype(jnp.float32)[:, None]
    weighted = (gate_col * hidden).astype(jnp.bfloat16)
    back_hidden = contract(grad_rows, weight_out, 1, 1)
    gate_grad = jnp.sum(back_hidden * hidden, axis=1)
    pre_grad = (gate_col * back_hidden * hidden_slope).astype(jnp.bfloat16)
    grad_out = contract(weighted, grad_rows, 0, 0)
    grad_in = contract(normed_rows, pre_grad, 0, 0)
    input_grad = contract(pre_grad, weight_in, 1, 1)
    return (input_grad, gate_grad, grad_in, grad_out)


def all_sum(part):
    devices = lax.axis_size("expert") * lax.axis_size("rep")
    flat = part.reshape(-1)
    width = -(-flat.shape[0] // (devices * 128)) * 128
    flat = jnp.pad(flat, (0, devices * width - flat.shape[0]))
    pieces = lax.all_to_all(
        flat.reshape(devices, width), ("expert", "rep"), split_axis=0, concat_axis=0, tiled=True
    )
    mine = jnp.sum(pieces, axis=0)
    whole = lax.all_gather(mine, ("expert", "rep"), axis=0, tiled=True)
    return whole.reshape(-1)[: part.size].reshape(part.shape)


def layer_body(
    tokens, grad_grid, keep_order, expert_ids, norm_gain, norm_bias, router_weight, w_in, w_out
):
    experts = router_weight.shape[1]
    tok_count = tokens.shape[0]
    model_width = tokens.shape[1]
    capacity = 5 * tok_count // (2 * experts)
    kept_count = tok_count // grad_grid.shape[0]
    lane = 128
    grad_kept = jnp.take_along_axis(grad_grid, keep_order[:, :kept_count, None], axis=1).reshape(
        tok_count, model_width
    )
    normed, inverse, normed_in = layer_norm(tokens, norm_gain, norm_bias)
    chosen, first_gate, second_gate = gate_values(normed_in, router_weight, expert_ids)
    gate_half = jnp.stack([first_gate, second_gate], axis=1).astype(jnp.bfloat16)
    expert_hits = jnp.sum(chosen, axis=1)
    before = jnp.cumsum(expert_hits, axis=0) - expert_hits
    slot_place = jnp.sum(before[:, None, :] * chosen, axis=2).astype(jnp.int32)
    slot_index = slot_place * experts + expert_ids
    slot_ids = jnp.arange(experts * capacity, dtype=jnp.int32)
    spread = (slot_index[:, :, None] == slot_ids[None, None, :]).astype(jnp.float32)
    assign = jnp.sum(spread, axis=1)
    assign_half = assign.astype(jnp.bfloat16)
    both = jnp.concatenate([normed_in, grad_kept], axis=1)
    send_gate = jnp.einsum(
        "tks,tk->s", spread, gate_half.astype(jnp.float32), precision=PRECISE
    ).astype(jnp.bfloat16)

    def send_part(low, high):
        rows = contract(assign_half[:, low * experts : high * experts], both, 0, 0)
        part_gate = send_gate[low * experts : high * experts]
        gate_block = jnp.concatenate(
            [part_gate[:, None], jnp.zeros((part_gate.shape[0], lane - 1), jnp.bfloat16)],
            axis=1,
        )
        whole = jnp.concatenate([rows.astype(jnp.bfloat16), gate_block], axis=1)
        return whole.reshape(high - low, experts, -1)

    rep_at = lax.axis_index("rep")
    copies = lax.axis_size("rep")
    cols = jnp.arange(lane, dtype=jnp.int32)[None, :]
    zero = jnp.zeros((), jnp.bfloat16)
    is_hi = cols == 2 * rep_at
    is_lo = cols == 2 * rep_at + 1
    half = capacity // 2
    bounds = ((0, half), (half, capacity))
    ret_parts, in_parts, out_parts = ([], [], [])
    for chunk, (low, high) in enumerate(bounds):
        got = lax.all_to_all(
            send_part(low, high), "expert", split_axis=1, concat_axis=1, tiled=True
        )
        got = lax.all_gather(got, "rep", axis=0, tiled=False)
        got = got.reshape(-1, got.shape[-1])
        weight_in, weight_out, at_hi, at_lo = (w_in[0], w_out[0], is_hi, is_lo)
        if chunk:
            weight_in, weight_out, at_hi, at_lo = lax.optimization_barrier(
                (weight_in, weight_out, at_hi, at_lo)
            )
        input_grad, gate_grad, grad_in, grad_out = expert_rows(
            got[:, :model_width],
            got[:, model_width : 2 * model_width],
            got[:, 2 * model_width],
            weight_in,
            weight_out,
        )
        in_parts.append(grad_in)
        out_parts.append(grad_out)
        rows_here = input_grad.shape[0]
        gate_hi = gate_grad.astype(jnp.bfloat16)
        gate_lo = (gate_grad - gate_hi.astype(jnp.float32)).astype(jnp.bfloat16)
        gate_cols = jnp.where(at_hi, gate_hi[:, None], jnp.where(at_lo, gate_lo[:, None], zero))
        packed = jnp.concatenate([input_grad.astype(jnp.bfloat16), gate_cols], axis=1)
        packed = packed.reshape(copies, rows_here // copies, -1)
        back = lax.psum_scatter(packed, "rep", scatter_dimension=0, tiled=True)
        back = back.reshape(high - low, experts, -1)
        ret_parts.append(lax.all_to_all(back, "expert", split_axis=1, concat_axis=1, tiled=True))
    ret = jnp.concatenate(ret_parts, axis=0).reshape(experts * capacity, -1)
    ret_rows = ret[:, :model_width].astype(jnp.float32)
    ret_gate = jnp.sum(
        ret[:, model_width : model_width + 2 * copies].astype(jnp.float32), axis=1
    )
    grad_in = in_parts[0] + in_parts[1]
    grad_out = out_parts[0] + out_parts[1]
    grad_w_in = grad_in[None]
    grad_w_out = grad_out[None]
    mixed_grad = jnp.dot(assign, ret_rows, precision=PRECISE)
    gate_grads = jnp.einsum("tks,s->tk", spread, ret_gate, precision=PRECISE)
    logit_grad = first_gate * second_gate * (gate_grads[:, 0] - gate_grads[:, 1])
    logits_grad = logit_grad[:, None] * (chosen[:, 0] - chosen[:, 1])
    normed_grad = mixed_grad + lax.dot_general(
        logits_grad, router_weight, (((1,), (1,)), ((), ())), precision=PRECISE
    )
    router_t = lax.dot_general(
        logits_grad, normed_in.astype(jnp.float32), (((0,), (0,)), ((), ())), precision=PRECISE
    )
    local_gain = jnp.sum(normed_grad * normed, axis=0)
    local_bias = jnp.sum(normed_grad, axis=0)
    summed = all_sum(jnp.concatenate([router_t.reshape(-1), local_gain, local_bias]))
    router_size = router_t.size
    grad_router = summed[:router_size].reshape(experts, model_width).T
    grad_gain = summed[router_size : router_size + model_width]
    grad_bias = summed[router_size + model_width :]
    scaled = normed_grad * norm_gain
    branch = inverse * (
        scaled
        - jnp.mean(scaled, axis=1, keepdims=True)
        - normed * jnp.mean(scaled * normed, axis=1, keepdims=True)
    )
    grad_tokens = (grad_kept.astype(jnp.float32) + branch).astype(jnp.bfloat16)
    return (grad_tokens, grad_w_in, grad_w_out, grad_router, grad_gain, grad_bias)


def solution(mesh):
    placed = (
        P(("expert", "rep"), None),
        P(("expert", "rep"), None, None),
        P(("expert", "rep"), None),
        P(("expert", "rep"), None),
        P(),
        P(),
        P(),
        P("expert", None, "rep"),
        P("expert", "rep", None),
    )
    return jax.shard_map(
        layer_body,
        mesh=mesh,
        in_specs=placed,
        out_specs=(
            P(("expert", "rep"), None),
            P("expert", None, "rep"),
            P("expert", "rep", None),
            P(),
            P(),
            P(),
        ),
        check_vma=False,
    )
```
